32 devices in a mesh: ens: 2 (over x), tile: 16 (over z, y, core).
Axes of the slice: x: 2, y: 2, z: 4, core: 2. Of those that a mesh axis runs over, the one named last changes fastest.
Arguments:
- atmosphere: bfloat16 [256, 256, 128], P(('ens', 'tile')), parts along dimension 0, may hold values from -6 to 6
- ocean_state: bfloat16 [4096, 512], P(('ens', 'tile')), parts along dimension 0, may hold values from -6 to 6
- land_sea: int32 [2048], P('tile'), may hold values 0 or 1
- owners: int32 [2048, 1], P('tile'), may hold values from 0 to 15; in each aligned block of 128 rows (0 to 127, 128 to 255, ...) at most 16 rows name the same one
- rotations: int32 [16], replicated, may hold values from 0 to 255
- conv_weight: bfloat16 [3, 9, 128, 128], replicated, may hold values from -0.1875 to 0.1875
- conv_bias: bfloat16 [3, 128], replicated, may hold values from -3 to 3
- force_weight: bfloat16 [128, 32], replicated, may hold values from -0.5 to 0.5
- ocean_weight: bfloat16 [16, 9, 64, 32], P('tile'), may hold values from -0.25 to 0.25
Outputs:
- atmos_out: bfloat16 [256, 256, 128], P(('ens', 'tile')), parts along dimension 0
- sea_state: bfloat16 [4096, 512], P(('ens', 'tile')), parts along dimension 0
The draws below stay inside these ranges and needn't reach their ends.
There are 2 independent parts, one for each index of `ens`. The reference program is written for one: setup_inputs(seed, part) draws one part's arguments, and reference() takes and returns one part's arrays. A program takes and returns all parts, laid end to end along the dimension named above; an argument that names none is the same for every part. Nothing has to cross between parts.
Inputs may be any that keep to these rules, and one draw needn't show every extreme that they name: `owners`: among the 128 blocks of one band no owner appears more than 16 times, and some owner appears exactly 16 times.
All inputs are finite; a program needn't handle non-finite values. No bound on the sum of `land_sea` on one device may be relied on, other than what follows from the above.
Results may differ from the reference program's by a relative error of at most 0.009.
Values may be sent and summed in bfloat16 or wider, within the bound.
No kernel may reach another device: no remote copies, remote signals or barrier semaphores. Data moves between devices by JAX's collectives and lax.ppermute only.
A program may use at most 64 MiB of HBM per device.

```python
import math
import jax
import jax.numpy as jnp
import numpy as np
from jax import lax

C = 128
OC = 32
BR = 8
LON = 256
LEADS = 2
LAYERS = 3
BH = 4
BW = 4
TILES = 16
ROWS = 128
NB = 128
BLOCKS = 2048
BLK = 512
CAP = 16


def set_ends(array, key, smallest, high):
    dims = array.shape
    index_at = [jax.random.randint(jax.random.fold_in(key, axis), (), 0, dims[axis]) for axis in range(len(dims))]
    array = array.at[tuple(index_at)].set(smallest)
    longest = dims.index(max(dims))
    index_at[longest] = (index_at[longest] + 1) % dims[longest]
    return array.at[tuple(index_at)].set(high)


def steps_of(stream_key, dims, cuts, smallest, high):
    def one(position, blocks):
        draws = jax.random.uniform(jax.random.fold_in(jax.random.fold_in(stream_key, 6), position), (blocks,), jnp.float32, smallest / len(cuts), high / len(cuts))
        return jnp.repeat(jnp.exp(draws), dims[position] // blocks).reshape((-1,) + (1,) * (len(dims) - position - 1))

    level = one(*cuts[0])
    for cut in cuts[1:]:
        level = level * one(*cut)
    return level


def deal_out(key, own, number, rows, number_of, top, bound, lean):
    sequence = jax.random.permutation(key, number_of)
    crowded, usual = shares(number_of, rows * top, bound, lean, True), shares(number_of, rows * top, bound, lean, False)
    places = jnp.arange(number_of)

    def named(tallies, offset_by):
        used = int((tallies > 0).sum())
        fixed = max(1, used // 4)
        passed = fixed + (places - fixed + offset_by * (used - fixed)) % max(1, number_of - fixed)
        return jnp.zeros((number_of,), jnp.int32).at[sequence[jnp.where(places < fixed, places, passed)]].set(jnp.asarray(tallies, jnp.int32))

    tallies = jnp.where(number % 4 == 0, named(crowded, number // 4), named(usual, number - number // 4 - 1))
    mixed = jax.random.permutation(jax.random.fold_in(own, 3), number_of)
    source_of, sink = mixed[0:number_of // 2 * 2:2], mixed[1:number_of // 2 * 2:2]
    room = jnp.minimum(tallies[source_of] - 1, bound - tallies[sink]) // 2
    room = jnp.where((source_of == sequence[0]) | (sink == sequence[0]) | (tallies[sink] == 0), 0, jnp.maximum(room, 0))
    passed = jax.random.randint(jax.random.fold_in(own, 4), (number_of // 2,), 0, 1 << 20) % (room + 1)
    tallies = tallies.at[source_of].add(-passed).at[sink].add(passed)
    labels = jnp.searchsorted(jnp.cumsum(tallies), jnp.arange(rows * top), side="right").astype(jnp.int32)
    table = labels.reshape(top, rows).T
    table = table[jax.random.permutation(jax.random.fold_in(own, 1), rows)]
    offset_by = jax.random.randint(jax.random.fold_in(own, 2), (rows, 1), 0, top)
    return jnp.take_along_axis(table, (jnp.arange(top)[None, :] + offset_by) % top, axis=1)


def shares(number_of, total, bound, lean, full):
    weights = [(1 << 20) // math.isqrt(rank ** lean) + 1 for rank in range(1, number_of + 1)]
    largest = bound if full else min(bound, max(-(-total // number_of), total * weights[0] // sum(weights)))
    least = 1 if total - largest >= number_of - 1 else 0
    holding, spare = [largest] + [least] * (number_of - 1), total - largest - least * (number_of - 1)
    while spare > 0:
        movable = [i for i in range(1, number_of) if holding[i] < largest] or [i for i in range(1, number_of) if holding[i] < bound]
        whole, budget = sum([weights[i] for i in movable]), spare
        for i in movable:
            more = min(bound - holding[i], max(1, budget * weights[i] // whole), spare)
            holding[i] = holding[i] + more
            spare = spare - more
    return np.array(holding)


def normal_values(key, extent, deviation, reach, cuts=(), kind=jnp.bfloat16):
    values = jax.random.normal(key, extent, jnp.float32) * deviation
    if len(cuts) > 0:
        values = steps_of(key, extent, cuts, -0.22, 0.18) * values
    return jnp.clip(values, min=-reach, max=reach).astype(kind)


def setup_inputs(seed: int = 0, part: int = 0) -> dict:
    seeds = jax.random.split(jax.random.key(seed), 10)
    part_splits = jax.random.split(jax.random.fold_in(seeds[9], part), 10)
    atmosphere = normal_values(part_splits[0], (ROWS, LON, C), 1.0, 6.0, ((0, 16),))
    ocean_state = normal_values(part_splits[1], (BLOCKS, BLK), 1.0, 6.0, ((0, 16),))
    land_sea = set_ends((jax.random.randint(seeds[2], (BLOCKS,), 0, 4) < 3).astype(jnp.int32), jax.random.fold_in(seeds[2], 1), 0, 1)
    owners_keys = jax.random.split(jax.random.fold_in(seeds[3], 1), BLOCKS // NB)
    owners_turns = jax.random.permutation(jax.random.fold_in(seeds[3], 3), BLOCKS // NB)
    owners = jax.vmap(lambda own, number: deal_out(jax.random.fold_in(seeds[3], 2), own, number, NB, TILES, 1, CAP, 2))(owners_keys, owners_turns).reshape((BLOCKS, 1))
    rotations = set_ends(jax.random.randint(seeds[4], (TILES,), 0, LON), jax.random.fold_in(seeds[4], 1), 0, LON - 1).astype(jnp.int32)
    conv_weight = normal_values(seeds[5], (LAYERS, 9, C, C), (9 * C) ** -0.5, 0.1875)
    conv_bias = normal_values(seeds[6], (LAYERS, C), 0.5, 3.0)
    force_weight = normal_values(seeds[7], (C, OC), C ** -0.5, 0.5)
    ocean_weight = normal_values(seeds[8], (TILES, 9, 2 * OC, OC), (18 * OC) ** -0.5, 0.25, ((0, 16),))
    return {"atmosphere": atmosphere, "ocean_state": ocean_state, "land_sea": land_sea, "owners": owners, "rotations": rotations, "conv_weight": conv_weight, "conv_bias": conv_bias, "force_weight": force_weight, "ocean_weight": ocean_weight}


def roll_one(band_rows, amount):
    return jnp.roll(band_rows, amount, axis=1)


def reference(atmosphere, ocean_state, land_sea, owners, rotations, conv_weight, conv_bias, force_weight, ocean_weight):
    channels = atmosphere.shape[2]
    ocean_ch = force_weight.shape[1]
    bands = atmosphere.reshape(TILES, BR, LON, channels)
    current = jax.vmap(roll_one)(bands, rotations).reshape(ROWS, LON, channels)
    outputs = []
    for lead_step in range(LEADS):
        for layer_index in range(LAYERS):
            dilation = 2 ** layer_index
            wrapped = jnp.concatenate([current[:, LON - dilation:], current, current[:, :dilation]], axis=1).astype(jnp.float32)
            kernel = conv_weight[layer_index].astype(jnp.float32).reshape(3, 3, channels, channels)
            convolved = lax.conv_general_dilated(
                wrapped[None], kernel, (1, 1), ((dilation, dilation), (0, 0)),
                rhs_dilation=(dilation, dilation),
                dimension_numbers=("NHWC", "HWIO", "NHWC"),
                precision=lax.Precision.HIGHEST)[0]
            current = (current.astype(jnp.float32) + jax.nn.gelu(convolved + conv_bias[layer_index].astype(jnp.float32))).astype(jnp.bfloat16)
        stored = jax.vmap(roll_one)(current.reshape(TILES, BR, LON, channels), -rotations)
        outputs.append(stored)
    atmos_out = outputs[-1].reshape(ROWS, LON, channels)
    summed = jnp.zeros((TILES * BR * LON, ocean_ch), jnp.float32)
    for stored in outputs:
        summed = summed + jnp.dot(stored.reshape(-1, channels), force_weight, preferred_element_type=jnp.float32)
    forcing = (0.5 * summed).astype(jnp.bfloat16)
    forcing = forcing.reshape(TILES, BR // BH, BH, LON // BW, BW, ocean_ch).transpose(0, 1, 3, 5, 2, 4)
    forcing = forcing.reshape(TILES, NB, ocean_ch, BH, BW)
    state_groups = ocean_state.reshape(TILES, NB, ocean_ch, BH, BW)
    owner_groups = owners.reshape(TILES, NB).astype(jnp.int32)
    sea_groups = land_sea.reshape(TILES, NB)

    def ocean_tile(pieces):
        forcing_blocks, state_blocks, owner_list, sea_flag = pieces
        kernels = ocean_weight[owner_list].astype(jnp.float32)
        joined = jnp.concatenate([forcing_blocks, state_blocks], axis=1).astype(jnp.float32)
        padded = jnp.pad(joined, ((0, 0), (0, 0), (1, 1), (1, 1)))
        total_sum = jnp.zeros((NB, ocean_ch, BH, BW), jnp.float32)
        for tap_row in range(3):
            for tap_col in range(3):
                window = padded[:, :, tap_row:tap_row + BH, tap_col:tap_col + BW]
                total_sum = total_sum + jnp.einsum("bcij,bco->boij", window, kernels[:, tap_row * 3 + tap_col], precision=lax.Precision.HIGHEST)
        updated = (state_blocks.astype(jnp.float32) + jax.nn.gelu(total_sum)).astype(jnp.bfloat16)
        updated = jnp.where(sea_flag[:, None, None, None] > 0, updated, jnp.zeros_like(updated))
        return updated.reshape(NB, ocean_ch * BH * BW)

    sea_state = lax.map(ocean_tile, (forcing, state_groups, owner_groups, sea_groups))
    return atmos_out, sea_state.reshape(BLOCKS, BLK)
```

```python
import functools

import jax
import jax.numpy as jnp
from jax import lax
from jax.experimental import pallas as pl
from jax.experimental.pallas import tpu as pltpu
from jax.sharding import PartitionSpec as P

LEADS = 2
LAYERS = 3
BH = 4
BW = 4
SUB = 16
PAD = 4
MARGIN = 2**LAYERS - 1
F32 = jnp.float32
BF16 = jnp.bfloat16
VMEM = pltpu.MemorySpace.VMEM
SMEM = pltpu.MemorySpace.SMEM


def gelu(x):
    half = 0.5 * x
    inner = x * (0.7978845608028654 + 0.035677408136300125 * (x * x))
    return half + half * jnp.tanh(inner)


def one_hot_columns(columns, shift, source_permuted, target_permuted):
    target = lax.broadcasted_iota(jnp.int32, (columns, columns), 0)
    source = lax.broadcasted_iota(jnp.int32, (columns, columns), 1)
    tiles = columns // SUB
    if target_permuted:
        target = (target % SUB) * tiles + target // SUB
    if source_permuted:
        source = (source % SUB) * tiles + source // SUB
    wanted = (target + shift) & (columns - 1)
    return jnp.where(wanted == source, 1.0, 0.0).astype(BF16)


def store_row(buf, row, value, reach):
    columns = value.shape[0]
    buf[row, PAD * SUB : PAD * SUB + columns, :] = value.astype(BF16)
    for k in range(reach):
        first = value[k * SUB : (k + 1) * SUB]
        at = PAD * SUB + columns + k * SUB
        buf[row, at : at + SUB, :] = pltpu.roll(first, SUB - 1, 0).astype(BF16)
        low = columns - (k + 1) * SUB
        last = value[low : low + SUB]
        at = PAD * SUB - (k + 1) * SUB
        buf[row, at : at + SUB, :] = pltpu.roll(last, 1, 0).astype(BF16)


def place_rows(buf, source, first_row, count, hot, reach, columns, source_at=0):
    for k in range(0, count, 2):
        pair = source[source_at + k]
        if k + 1 < count:
            pair = jnp.concatenate([pair, source[source_at + k + 1]], axis=1)
        moved = jnp.dot(hot, pair, preferred_element_type=F32)
        store_row(buf, first_row + k, moved[:, :128], reach)
        if k + 1 < count:
            store_row(buf, first_row + k + 1, moved[:, 128:], reach)


def conv_layer(src, dst, weights, bias, layer, groups, reach, inside, columns):
    dilation = 2**layer
    offset = bias[layer][None, :].astype(F32)

    def pair_at(row):
        pieces = []
        for rho in range(4):
            for tap in range(3):
                start = (PAD + (tap - 1) * dilation) * SUB
                pieces.append(src[row + (rho - 1) * dilation, start : start + columns, :])
        summed = jnp.dot(
            jnp.concatenate(pieces, axis=1), weights[layer], preferred_element_type=F32
        )
        for half in range(2):
            at = row + half * dilation
            kept = src[at, PAD * SUB : PAD * SUB + columns, :].astype(F32)
            value = kept + gelu(summed[:, half * 128 : half * 128 + 128] + offset)
            if inside is not None:
                value = value * inside(at)
            store_row(dst, at, value, reach)

    for first, step, count in groups:

        def body(k, carry, first=first, step=step):
            pair_at(first + k * step)
            return carry

        lax.fori_loop(0, count, body, 0)


def lead_rows(buf_a, buf_b, weights, bias, info, band_rows, columns):
    low = info[2].astype(F32)
    high = info[3].astype(F32)

    def inside(row):
        return jnp.where(row < MARGIN, low, jnp.where(row >= MARGIN + band_rows, high, 1.0))

    conv_layer(buf_a, buf_b, weights, bias, 0, [(1, 2, 10)], 2, inside, columns)
    conv_layer(buf_b, buf_a, weights, bias, 1, [(3, 4, 4), (4, 4, 4)], 4, inside, columns)
    conv_layer(buf_a, buf_b, weights, bias, 2, [(MARGIN, 1, 4)], 0, None, columns)


def prep_kernel(own, conv_weight, field, weights):
    columns = own.shape[1]
    hot = one_hot_columns(columns, 0, False, True)
    place_rows(field, own, 0, own.shape[0], hot, 1, columns)
    weights[...] = jnp.zeros_like(weights)
    for layer in range(LAYERS):
        for tap_row in range(3):
            for tap in range(3):
                tile = conv_weight[layer, tap_row * 3 + tap]
                for half in range(2):
                    at = ((tap_row + half) * 3 + tap) * 128
                    weights[layer, at : at + 128, half * 128 : half * 128 + 128] = tile


def lead_one_kernel(info, own, up, down, weights, bias, field, send_up, send_down, buf_a, buf_b):
    band_rows, columns = own.shape[0], up.shape[1]
    buf_a[MARGIN : MARGIN + band_rows] = own[...]
    hot = one_hot_columns(columns, info[0], False, True)
    place_rows(buf_a, up, 0, MARGIN, hot, 1, columns)
    hot = one_hot_columns(columns, info[1], False, True)
    place_rows(buf_a, down, MARGIN + band_rows, MARGIN, hot, 1, columns)
    lead_rows(buf_a, buf_b, weights, bias, info, band_rows, columns)
    for row in range(band_rows):
        value = buf_b[MARGIN + row, PAD * SUB : PAD * SUB + columns, :]
        store_row(field, row, value.astype(F32), 1)
        if row < MARGIN:
            send_down[row] = value
        if row >= band_rows - MARGIN:
            send_up[row - (band_rows - MARGIN)] = value


def table_kernel(gathered, table):
    lanes_from = lax.broadcasted_iota(jnp.int32, (128, 512), 0)
    lanes_to = lax.broadcasted_iota(jnp.int32, (128, 512), 1)
    cell = lanes_to // 128
    spread = jnp.where(lanes_to % 128 - lanes_from == 32 * (cell - 1), 1.0, 0.0).astype(BF16)

    def body(owner, carry):
        for tap_row in range(3):
            wide = jnp.dot(gathered[owner, tap_row], spread, preferred_element_type=F32)
            for half in range(2):
                for q in range(4):
                    at = tap_row * 256 + half * 128 + q * 32
                    table[owner, at : at + 32, :] = wide[
                        half * 32 : half * 32 + 32, q * 128 : q * 128 + 128
                    ].astype(BF16)
        return carry

    lax.fori_loop(0, gathered.shape[0], body, 0)


def block_lanes(channel_major_rows):
    a = lax.broadcasted_iota(jnp.int32, (512, 512), 0)
    b = lax.broadcasted_iota(jnp.int32, (512, 512), 1)
    src, dst = (a, b) if channel_major_rows else (b, a)
    wanted = (dst % 32) * 16 + dst // 32
    return jnp.where(src == wanted, 1.0, 0.0).astype(BF16)


def lead_two_kernel(
    info, own, up, down, weights, bias, force, table, state, owners, sea,
    atmos_out, sea_state, buf_a, buf_b, joined, acc,
):
    band_rows, columns = own.shape[0], up.shape[1]
    buf_a[MARGIN : MARGIN + band_rows] = own[...]
    hot = one_hot_columns(columns, info[0], True, True)
    place_rows(buf_a, up, 0, MARGIN, hot, 1, columns)
    hot = one_hot_columns(columns, info[1], True, True)
    place_rows(buf_a, down, MARGIN + band_rows, MARGIN, hot, 1, columns)
    lead_rows(buf_a, buf_b, weights, bias, info, band_rows, columns)
    hot = one_hot_columns(columns, 0, True, False)
    for row in range(0, band_rows, 2):
        pair = [
            buf_b[MARGIN + row + k, PAD * SUB : PAD * SUB + columns, :] for k in range(2)
        ]
        moved = jnp.dot(hot, jnp.concatenate(pair, axis=1), preferred_element_type=F32)
        atmos_out[row] = moved[:, :128].astype(BF16)
        atmos_out[row + 1] = moved[:, 128:].astype(BF16)

    blocks = band_rows // BH * (columns // BW)
    per_half = columns // BW
    wide = force[...]
    zero = jnp.zeros((128, 32), BF16)
    spread = jnp.concatenate(
        [
            jnp.concatenate([wide if q == p else zero for p in range(4)], axis=1)
            for q in range(4)
        ],
        axis=0,
    )
    spread = jnp.concatenate([spread, spread], axis=0)
    forcing = []
    for i in range(BH):
        pieces = []
        for half in range(band_rows // BH):
            row = half * BH + i
            for g in range(SUB // BW):
                cells = []
                for field, at in ((own, row), (buf_b, MARGIN + row)):
                    for q in range(BW):
                        tile = (PAD + g * BW + q) * SUB
                        cells.append(field[at, tile : tile + SUB, :])
                pieces.append(jnp.concatenate(cells, axis=1))
        wide = jnp.concatenate(pieces, axis=0)
        forcing.append(
            (0.5 * jnp.dot(wide, spread, preferred_element_type=F32)).astype(BF16)
        )
    forcing = jnp.concatenate(forcing, axis=1)
    a = lax.broadcasted_iota(jnp.int32, (blocks, blocks), 0)
    b = lax.broadcasted_iota(jnp.int32, (blocks, blocks), 1)
    source = (a // per_half) * per_half + (a % 4) * SUB + (a % per_half) // 4
    order = jnp.where(source == b, 1.0, 0.0).astype(BF16)
    forcing = jnp.dot(order, forcing, preferred_element_type=F32).astype(BF16)
    own_state = jnp.dot(
        state[...], block_lanes(True), preferred_element_type=F32
    ).astype(BF16)
    joined[...] = jnp.zeros_like(joined)
    for i in range(BH):
        for tap_row in range(3):
            at = i + tap_row - 1
            if 0 <= at < BH:
                here = pl.ds(i * blocks, blocks)
                joined[here, tap_row * 256 : tap_row * 256 + 128] = forcing[
                    :, at * 128 : at * 128 + 128
                ]
                joined[here, tap_row * 256 + 128 : tap_row * 256 + 256] = own_state[
                    :, at * 128 : at * 128 + 128
                ]
    owner = jnp.broadcast_to(owners[...], (blocks, 128))

    def body(k, carry):
        pair = jnp.concatenate([table[2 * k], table[2 * k + 1]], axis=1)
        for i in range(BH):
            here = pl.ds(i * blocks, blocks)
            got = jnp.dot(joined[here, :], pair, preferred_element_type=F32)
            old = acc[here, :]
            new = jnp.where(owner == 2 * k, got[:, :128], old)
            acc[here, :] = jnp.where(owner == 2 * k + 1, got[:, 128:], new)
        return carry

    acc[...] = jnp.zeros_like(acc)
    lax.fori_loop(0, table.shape[0] // 2, body, 0)
    fresh = []
    for i in range(BH):
        kept = own_state[:, i * 128 : i * 128 + 128].astype(F32)
        fresh.append((kept + gelu(acc[i * blocks : (i + 1) * blocks, :])).astype(BF16))
    result = jnp.dot(
        jnp.concatenate(fresh, axis=1), block_lanes(False), preferred_element_type=F32
    )
    flag = jnp.broadcast_to(sea[...], (blocks, 512))
    sea_state[...] = jnp.where(flag > 0, result, 0.0).astype(BF16)


def call(kernel, out_shape, scratch, specs, name):
    return pl.pallas_call(
        kernel,
        out_shape=out_shape,
        in_specs=[pl.BlockSpec(memory_space=s) for s in specs],
        out_specs=jax.tree.map(lambda _: pl.BlockSpec(memory_space=VMEM), out_shape),
        scratch_shapes=scratch,
        name=name,
        compiler_params=pltpu.CompilerParams(vmem_limit_bytes=56 * 2**20),
    )


def local(
    atmosphere, ocean_state, land_sea, owners, rotations,
    conv_weight, conv_bias, force_weight, ocean_weight,
):
    tile = lax.axis_index("tile")
    tiles = lax.axis_size("tile")
    band_rows, columns, channels = atmosphere.shape
    blocks = owners.shape[0]
    shape = jax.ShapeDtypeStruct
    up_pairs = [(i, i + 1) for i in range(tiles - 1)]
    down_pairs = [(j, i) for i, j in up_pairs]

    own_shift = rotations[tile]
    up_shift = own_shift - rotations[jnp.maximum(tile - 1, 0)]
    down_shift = own_shift - rotations[jnp.minimum(tile + 1, tiles - 1)]
    info = jnp.stack(
        [up_shift, down_shift, (tile > 0).astype(jnp.int32), (tile < tiles - 1).astype(jnp.int32)]
    ).astype(jnp.int32)

    up = lax.ppermute(atmosphere[band_rows - MARGIN :], "tile", up_pairs)
    down = lax.ppermute(atmosphere[:MARGIN], "tile", down_pairs)

    taps = ocean_weight[0].reshape(3, 3, 64, 32)
    strip = jnp.concatenate(
        [taps[:, 2], taps[:, 1], taps[:, 0], jnp.zeros_like(taps[:, 0])], axis=-1
    )
    gathered = lax.all_to_all(
        jnp.broadcast_to(strip[None], (tiles, 3, 64, 128)), "tile", 0, 0, tiled=True
    )

    padded = columns + 2 * PAD * SUB
    field_shape = shape((band_rows, padded, channels), BF16)
    own, weights = call(
        prep_kernel,
        (field_shape, shape((LAYERS, 1536, 256), BF16)),
        [], [VMEM] * 2, "prep",
    )(atmosphere, conv_weight)

    buffers = [pltpu.VMEM((band_rows + 2 * MARGIN, padded, channels), BF16)] * 2
    halo = shape((MARGIN, columns, channels), BF16)
    lead_one, send_up, send_down = call(
        lead_one_kernel, (field_shape, halo, halo), buffers, [SMEM] + [VMEM] * 5, "lead_one"
    )(info, own, up, down, weights, conv_bias)

    up = lax.ppermute(send_up, "tile", up_pairs)
    down = lax.ppermute(send_down, "tile", down_pairs)

    table = call(
        table_kernel, shape((tiles, 768, 128), BF16), [], [VMEM], "table"
    )(gathered)

    return call(
        lead_two_kernel,
        (shape(atmosphere.shape, BF16), shape(ocean_state.shape, BF16)),
        buffers
        + [pltpu.VMEM((BH * blocks, 768), BF16), pltpu.VMEM((BH * blocks, 128), F32)],
        [SMEM] + [VMEM] * 10, "lead_two",
    )(
        info, lead_one, up, down, weights, conv_bias, force_weight, table,
        ocean_state, owners, land_sea[:, None],
    )


def solution(mesh):
    in_specs = (
        P(("ens", "tile"), None, None),
        P(("ens", "tile"), None),
        P("tile"),
        P("tile", None),
        P(),
        P(),
        P(),
        P(),
        P("tile", None, None, None),
    )
    out_specs = (P(("ens", "tile"), None, None), P(("ens", "tile"), None))
    return jax.shard_map(local, mesh=mesh, in_specs=in_specs, out_specs=out_specs, check_vma=False)
```

```python
import jax
import jax.numpy as jnp
from jax import lax
from jax.experimental import pallas as pl
from jax.experimental.pallas import tpu as pltpu
from jax.sharding import PartitionSpec as P


LAYERS = 3
BH = 4
BW = 4
SUB = 16
PAD = 4
GROUP = 2
MARGIN = 2**LAYERS - 1
F32 = jnp.float32
BF16 = jnp.bfloat16
VMEM = pltpu.MemorySpace.VMEM
SMEM = pltpu.MemorySpace.SMEM


def gelu(x):
    half = 0.5 * x
    inner = x * (0.7978845608028654 + 0.035677408136300125 * (x * x))
    return half + half * jnp.tanh(inner)


def one_hot_columns(columns, shift, source_permuted, target_permuted):
    target = lax.broadcasted_iota(jnp.int32, (columns, columns), 0)
    source = lax.broadcasted_iota(jnp.int32, (columns, columns), 1)
    tiles = columns // SUB
    if target_permuted:
        target = (target % SUB) * tiles + target // SUB
    if source_permuted:
        source = (source % SUB) * tiles + source // SUB
    wanted = (target + shift) & (columns - 1)
    return jnp.where(wanted == source, 1.0, 0.0).astype(BF16)


def store_row(ref, row, value, reach):
    columns = value.shape[0]
    ref[row, PAD * SUB : PAD * SUB + columns, :] = value.astype(BF16)
    for k in range(reach):
        first = value[k * SUB : (k + 1) * SUB]
        at = PAD * SUB + columns + k * SUB
        ref[row, at : at + SUB, :] = pltpu.roll(first, SUB - 1, 0).astype(BF16)
        low = columns - (k + 1) * SUB
        last = value[low : low + SUB]
        at = PAD * SUB - (k + 1) * SUB
        ref[row, at : at + SUB, :] = pltpu.roll(last, 1, 0).astype(BF16)


def place_rows(ref, source, hot, reach):
    count = source.shape[0]
    for k in range(0, count, 2):
        pair = source[k]
        if k + 1 < count:
            pair = jnp.concatenate([pair, source[k + 1]], axis=1)
        moved = jnp.dot(hot, pair, preferred_element_type=F32)
        store_row(ref, k, moved[:, :128], reach)
        if k + 1 < count:
            store_row(ref, k + 1, moved[:, 128:], reach)


def layer_rows(layer, band_rows):
    used = 2 ** (layer + 1) - 1
    return list(range(used, band_rows + 2 * MARGIN - used))


def row_groups(layer, band_rows, size):
    rows = set(layer_rows(layer, band_rows))
    firsts = []
    while rows:
        r = min(rows)
        firsts.append(r)
        rows -= {r, r + 2**layer}
    return [firsts[k : k + size] for k in range(0, len(firsts), size)]


def lead_rows(source, middle, sink, weights, bias, limits, results, band_rows, columns):
    low, high = limits
    steps = [
        (layer, group)
        for layer in range(LAYERS)
        for group in row_groups(layer, band_rows, GROUP)
    ]
    places = [source, middle[0], middle[1]]

    def product(layer, group, out):
        dilation = 2**layer
        stacked = []
        for first in group:
            pieces = []
            for rho in range(4):
                ref, row = places[layer](first + (rho - 1) * dilation)
                for tap in range(3):
                    start = (PAD + (tap - 1) * dilation) * SUB
                    pieces.append(ref[row, start : start + columns, :])
            stacked.append(jnp.concatenate(pieces, axis=1))
        out[: len(group) * columns, :] = jnp.dot(
            jnp.concatenate(stacked, axis=0), weights[layer], preferred_element_type=F32
        )

    def finish(layer, group, got):
        offset = bias[layer][None, :].astype(F32)
        for k, first in enumerate(group):
            for half in range(2):
                at = first + half * 2**layer
                ref, row = places[layer](at)
                kept = ref[row, PAD * SUB : PAD * SUB + columns, :].astype(F32)
                summed = got[k * columns : (k + 1) * columns, half * 128 : half * 128 + 128]
                value = kept + gelu(summed + offset)
                if layer + 1 == LAYERS:
                    sink(at, value)
                    continue
                if at < MARGIN:
                    value = value * low
                elif at >= MARGIN + band_rows:
                    value = value * high
                ref, row = places[layer + 1](at)
                store_row(ref, row, value, 2 ** (layer + 1))

    for k, (layer, group) in enumerate(steps):
        if k and steps[k - 1][0] == layer:
            product(layer, group, results.at[k % 2])
            finish(*steps[k - 1], results.at[(k - 1) % 2])
        else:
            if k:
                finish(*steps[k - 1], results.at[(k - 1) % 2])
            product(layer, group, results.at[k % 2])
    finish(*steps[-1], results.at[(len(steps) - 1) % 2])


def shifts(rotations):
    tile = lax.axis_index("tile")
    tiles = rotations.shape[0]
    own = rotations[tile]
    up = own - rotations[jnp.maximum(tile - 1, 0)]
    down = own - rotations[jnp.minimum(tile + 1, tiles - 1)]
    low = jnp.where(tile > 0, 1.0, 0.0).astype(F32)
    high = jnp.where(tile < tiles - 1, 1.0, 0.0).astype(F32)
    return up, down, (low, high)


def run_lead(
    rotations, own, up, down, weights, bias, up_buf, down_buf, mid_a, mid_b, results, sink, permuted
):
    band_rows, columns = own.shape[0], up.shape[1]
    up_shift, down_shift, limits = shifts(rotations)
    place_rows(up_buf, up, one_hot_columns(columns, up_shift, permuted, True), 1)
    place_rows(down_buf, down, one_hot_columns(columns, down_shift, permuted, True), 1)

    def source(e):
        if e < MARGIN:
            return up_buf, e
        if e < MARGIN + band_rows:
            return own, e - MARGIN
        return down_buf, e - MARGIN - band_rows

    lead_rows(
        source, [lambda e: (mid_a, e), lambda e: (mid_b, e)], sink,
        weights, bias, limits, results, band_rows, columns,
    )


def prep_kernel(own, conv_weight, ocean_weight, field, weights, packed):
    columns = own.shape[1]
    half_rows = ocean_weight.shape[0] // 2
    pack = jnp.concatenate([ocean_weight[:half_rows], ocean_weight[half_rows:]], axis=1)

    def copy(k, carry):
        packed[k] = pack
        return carry

    lax.fori_loop(0, packed.shape[0], copy, 0)
    place_rows(field, own, one_hot_columns(columns, 0, False, True), 1)
    zero = jnp.zeros((384, 128), BF16)
    for layer in range(LAYERS):
        for half in range(2):
            at = (1 - half) * 1152
            weights[layer, at : at + 384, half * 128 : half * 128 + 128] = zero
            for tap in range(9):
                at = half * 384 + tap * 128
                weights[layer, at : at + 128, half * 128 : half * 128 + 128] = conv_weight[
                    layer, tap
                ]


def lead_one_kernel(
    rotations, own, up, down, weights, bias, field, send_up, send_down, *scratch
):
    band_rows = own.shape[0]

    def sink(e, value):
        row = e - MARGIN
        store_row(field, row, value, 1)
        if row < MARGIN:
            send_down[row] = value.astype(BF16)
        if row >= band_rows - MARGIN:
            send_up[row - (band_rows - MARGIN)] = value.astype(BF16)

    run_lead(rotations, own, up, down, weights, bias, *scratch, sink, False)


def table_kernel(gathered, table):
    taps_from = lax.broadcasted_iota(jnp.int32, (96, 512), 0)
    lanes_to = lax.broadcasted_iota(jnp.int32, (96, 512), 1)
    cell = lanes_to // 128
    spread = jnp.where(
        lanes_to % 128 + 32 * (taps_from // 32) - taps_from % 32 == 32 * (cell + 1), 1.0, 0.0
    ).astype(BF16)

    def body(owner, carry):
        pack = gathered[owner]
        taps = jnp.concatenate([pack[:, :64], pack[:, 64:]], axis=0)
        for tap_row in range(3):
            wide = lax.dot_general(
                taps[tap_row * 96 : tap_row * 96 + 96], spread, (((0,), (0,)), ((), ())),
                preferred_element_type=F32,
            )
            for half in range(2):
                for q in range(4):
                    at = tap_row * 256 + half * 128 + q * 32
                    table[owner, at : at + 32, :] = wide[
                        half * 32 : half * 32 + 32, q * 128 : q * 128 + 128
                    ].astype(BF16)
        return carry

    lax.fori_loop(0, gathered.shape[0], body, 0)


def block_lanes(channel_major_rows):
    a = lax.broadcasted_iota(jnp.int32, (512, 512), 0)
    b = lax.broadcasted_iota(jnp.int32, (512, 512), 1)
    src, dst = (a, b) if channel_major_rows else (b, a)
    wanted = (dst % 32) * 16 + dst // 32
    return jnp.where(src == wanted, 1.0, 0.0).astype(BF16)


def lead_two_kernel(
    rotations, own, up, down, weights, bias, force, table, state, owners, sea,
    atmos_out, sea_state, last, joined, acc, *scratch,
):
    band_rows, columns = own.shape[0], up.shape[1]

    def sink(e, value):
        last[e - MARGIN] = value.astype(BF16)

    run_lead(rotations, own, up, down, weights, bias, *scratch, sink, True)
    hot = one_hot_columns(columns, 0, True, False)
    for row in range(0, band_rows, 2):
        moved = jnp.dot(
            hot, jnp.concatenate([last[row], last[row + 1]], axis=1), preferred_element_type=F32
        )
        atmos_out[row] = moved[:, :128].astype(BF16)
        atmos_out[row + 1] = moved[:, 128:].astype(BF16)

    blocks = band_rows // BH * (columns // BW)
    per_half = columns // BW
    wide = force[...]
    zero = jnp.zeros((32, 128), BF16)
    spread = jnp.concatenate(
        [
            jnp.concatenate([wide if q % 4 == p else zero for q in range(8)], axis=1)
            for p in range(4)
        ],
        axis=0,
    )
    forcing = []
    for i in range(BH):
        pieces = []
        for half in range(band_rows // BH):
            row = half * BH + i
            for g in range(SUB // BW):
                cells = []
                for field, pad in ((own, PAD), (last, 0)):
                    for q in range(BW):
                        tile = (pad + g * BW + q) * SUB
                        cells.append(field[row, tile : tile + SUB, :])
                pieces.append(jnp.concatenate(cells, axis=1))
        wide = jnp.concatenate(pieces, axis=0)
        forcing.append(
            (
                0.5
                * lax.dot_general(
                    wide, spread, (((1,), (1,)), ((), ())), preferred_element_type=F32
                )
            ).astype(BF16)
        )
    forcing = jnp.concatenate(forcing, axis=1)
    a = lax.broadcasted_iota(jnp.int32, (blocks, blocks), 0)
    b = lax.broadcasted_iota(jnp.int32, (blocks, blocks), 1)
    source = (a // per_half) * per_half + (a % 4) * SUB + (a % per_half) // 4
    order = jnp.where(source == b, 1.0, 0.0).astype(BF16)
    forcing = jnp.dot(order, forcing, preferred_element_type=F32).astype(BF16)
    own_state = jnp.dot(
        state[...], block_lanes(True), preferred_element_type=F32
    ).astype(BF16)
    joined[...] = jnp.zeros_like(joined)
    for i in range(BH):
        for tap_row in range(3):
            at = i + tap_row - 1
            if 0 <= at < BH:
                here = pl.ds(i * blocks, blocks)
                joined[here, tap_row * 256 : tap_row * 256 + 128] = forcing[
                    :, at * 128 : at * 128 + 128
                ]
                joined[here, tap_row * 256 + 128 : tap_row * 256 + 256] = own_state[
                    :, at * 128 : at * 128 + 128
                ]
    owner = jnp.transpose(jnp.broadcast_to(owners[...], (128, blocks)))

    def body(k, carry):
        pair = jnp.concatenate([table[2 * k], table[2 * k + 1]], axis=1)
        for i in range(BH):
            here = pl.ds(i * blocks, blocks)
            got = jnp.dot(joined[here, :], pair, preferred_element_type=F32)
            old = acc[here, :]
            new = jnp.where(owner == 2 * k, got[:, :128], old)
            acc[here, :] = jnp.where(owner == 2 * k + 1, got[:, 128:], new)
        return carry

    acc[...] = jnp.zeros_like(acc)
    lax.fori_loop(0, table.shape[0] // 2, body, 0)
    fresh = []
    for i in range(BH):
        kept = own_state[:, i * 128 : i * 128 + 128].astype(F32)
        fresh.append((kept + gelu(acc[i * blocks : (i + 1) * blocks, :])).astype(BF16))
    result = jnp.dot(
        jnp.concatenate(fresh, axis=1), block_lanes(False), preferred_element_type=F32
    )
    flag = jnp.transpose(jnp.broadcast_to(sea[...], (128, blocks))) > 0
    for i in range(BH):
        lanes = slice(i * 128, i * 128 + 128)
        sea_state[:, lanes] = jnp.where(flag, result[:, lanes], 0.0).astype(BF16)


def call(kernel, out_shape, scratch, specs, limit):
    return pl.pallas_call(
        kernel,
        out_shape=out_shape,
        in_specs=[pl.BlockSpec(memory_space=s) for s in specs],
        out_specs=jax.tree.map(lambda _: pl.BlockSpec(memory_space=VMEM), out_shape),
        scratch_shapes=scratch,
        compiler_params=pltpu.CompilerParams(vmem_limit_bytes=limit * 2**20),
    )


def here(x):
    return pltpu.with_memory_space_constraint(x, VMEM)


def local(
    atmosphere, ocean_state, land_sea, owners, rotations,
    conv_weight, conv_bias, force_weight, ocean_weight,
):
    tiles = lax.axis_size("tile")
    band_rows, columns, channels = atmosphere.shape
    blocks = owners.shape[0]
    shape = jax.ShapeDtypeStruct
    up_pairs = [(i, i + 1) for i in range(tiles - 1)]
    down_pairs = [(j, i) for i, j in up_pairs]

    up = lax.ppermute(atmosphere[band_rows - MARGIN :], "tile", up_pairs)
    down = lax.ppermute(atmosphere[:MARGIN], "tile", down_pairs)

    padded = columns + 2 * PAD * SUB
    own, weights, packed = call(
        prep_kernel,
        (
            pltpu.VMEM((band_rows, padded, channels), BF16),
            pltpu.VMEM((LAYERS, 1536, 256), BF16),
            pltpu.VMEM((tiles, 144, 128), BF16),
        ),
        [], [VMEM] * 3, 12,
    )(atmosphere, conv_weight, jnp.swapaxes(ocean_weight[0], 1, 2).reshape(-1, 64))
    own, weights = here(own), here(weights)
    gathered = lax.all_to_all(packed, "tile", 0, 0, tiled=True)

    scratch = [
        pltpu.VMEM((MARGIN, padded, channels), BF16),
        pltpu.VMEM((MARGIN, padded, channels), BF16),
        pltpu.VMEM((band_rows + 2 * MARGIN, padded, channels), BF16),
        pltpu.VMEM((band_rows + 2 * MARGIN, padded, channels), BF16),
        pltpu.VMEM((2, GROUP * columns, 256), F32),
    ]
    halo = pltpu.VMEM((MARGIN, columns, channels), BF16)
    lead_one, send_up, send_down = call(
        lead_one_kernel,
        (pltpu.VMEM((band_rows, padded, channels), BF16), halo, halo),
        scratch, [SMEM] + [VMEM] * 5, 16,
    )(rotations, own, here(up), here(down), weights, conv_bias)

    up = lax.ppermute(send_up, "tile", up_pairs)
    down = lax.ppermute(send_down, "tile", down_pairs)

    table = call(table_kernel, pltpu.VMEM((tiles, 768, 128), BF16), [], [VMEM], 8)(here(gathered))

    return call(
        lead_two_kernel,
        (shape(atmosphere.shape, BF16), shape(ocean_state.shape, BF16)),
        [
            pltpu.VMEM((band_rows, columns, channels), BF16),
            pltpu.VMEM((BH * blocks, 768), BF16),
            pltpu.VMEM((BH * blocks, 128), F32),
        ]
        + scratch,
        [SMEM] + [VMEM] * 10, 20,
    )(
        rotations, here(lead_one), here(up), here(down), weights, conv_bias, force_weight.T, here(table),
        ocean_state, owners.reshape(1, blocks), land_sea.reshape(1, blocks),
    )


def solution(mesh):
    in_specs = (
        P(("ens", "tile"), None, None),
        P(("ens", "tile"), None),
        P("tile"),
        P("tile", None),
        P(),
        P(),
        P(),
        P(),
        P("tile", None, None, None),
    )
    out_specs = (P(("ens", "tile"), None, None), P(("ens", "tile"), None))

    return jax.shard_map(local, mesh=mesh, in_specs=in_specs, out_specs=out_specs, check_vma=False)
```

```python
import jax
import jax.numpy as jnp
from jax import lax
from jax.experimental import pallas as pl
from jax.experimental.pallas import tpu as pltpu
from jax.sharding import PartitionSpec as P


LAYERS = 3
BH = 4
BW = 4
SUB = 16
PAD = 4
GROUP = 2
MARGIN = 2**LAYERS - 1
F32 = jnp.float32
BF16 = jnp.bfloat16
VMEM = pltpu.MemorySpace.VMEM
SMEM = pltpu.MemorySpace.SMEM


def gelu(x):
    half = 0.5 * x
    inner = x * (0.7978845608028654 + 0.035677408136300125 * (x * x))
    return half + half * jnp.tanh(inner)


def one_hot_columns(columns, shift, source_permuted, target_permuted):
    target = lax.broadcasted_iota(jnp.int32, (columns, columns), 0)
    source = lax.broadcasted_iota(jnp.int32, (columns, columns), 1)
    tiles = columns // SUB
    if target_permuted:
        target = (target % SUB) * tiles + target // SUB
    if source_permuted:
        source = (source % SUB) * tiles + source // SUB
    wanted = (target + shift) & (columns - 1)
    return jnp.where(wanted == source, 1.0, 0.0).astype(BF16)


def store_row(ref, row, value, reach):
    columns = value.shape[0]
    ref[row, PAD * SUB : PAD * SUB + columns, :] = value.astype(BF16)
    for k in range(reach):
        first = value[k * SUB : (k + 1) * SUB]
        at = PAD * SUB + columns + k * SUB
        ref[row, at : at + SUB, :] = pltpu.roll(first, SUB - 1, 0).astype(BF16)
        low = columns - (k + 1) * SUB
        last = value[low : low + SUB]
        at = PAD * SUB - (k + 1) * SUB
        ref[row, at : at + SUB, :] = pltpu.roll(last, 1, 0).astype(BF16)


def layer_rows(layer, band_rows):
    used = 2 ** (layer + 1) - 1
    return list(range(used, band_rows + 2 * MARGIN - used))


def row_groups(rows, dilation, size):
    rows = set(rows)
    firsts = []
    while rows:
        r = min(rows)
        firsts.append(r)
        rows -= {r, r + dilation}
    return [firsts[k : k + size] for k in range(0, len(firsts), size)]


def rotate_kernel(rotations, own, field, send_up, send_down):
    band_rows, columns = own.shape[0], own.shape[1]
    hot = one_hot_columns(columns, -rotations[lax.axis_index("tile")], False, True)
    for k in range(0, band_rows, 2):
        moved = jnp.dot(
            hot, jnp.concatenate([own[k], own[k + 1]], axis=1), preferred_element_type=F32
        )
        for half in range(2):
            give_row(k + half, moved[:, half * 128 : half * 128 + 128], field, send_up, send_down)


def give_row(row, value, field, send_up, send_down):
    band_rows = field.shape[0]
    store_row(field, row, value, 1)
    if row < MARGIN:
        send_down[row] = value.astype(BF16)
    if row >= band_rows - MARGIN:
        send_up[row - (band_rows - MARGIN)] = value.astype(BF16)


def pack_kernel(ocean_weight, packed):
    half_rows = ocean_weight.shape[0] // 2
    pack = jnp.concatenate([ocean_weight[:half_rows], ocean_weight[half_rows:]], axis=1)

    def copy(k, carry):
        packed[k] = pack
        return carry

    lax.fori_loop(0, packed.shape[0], copy, 0)


def pair_weights(conv_weight, weights):
    zero = jnp.zeros((384, 128), BF16)
    for layer in range(LAYERS):
        for half in range(2):
            at = (1 - half) * 1152
            weights[layer, at : at + 384, half * 128 : half * 128 + 128] = zero
            for tap in range(9):
                at = half * 384 + tap * 128
                weights[layer, at : at + 128, half * 128 : half * 128 + 128] = conv_weight[
                    layer, tap
                ]


def conv_rows(plan, place, sink, weights, bias, results, band_rows, columns):
    tile = lax.axis_index("tile")
    low = jnp.where(tile > 0, 1.0, 0.0).astype(F32)
    high = jnp.where(tile < lax.axis_size("tile") - 1, 1.0, 0.0).astype(F32)

    def piece(ref, row, moved):
        padded = ref.shape[1] > columns
        if padded or moved == 0:
            start = (PAD * SUB if padded else 0) + moved * SUB
            return ref[row, start : start + columns, :]
        edge = ref[row, columns - SUB :, :] if moved < 0 else ref[row, :SUB, :]
        edge = pltpu.roll(edge.astype(F32), 1 if moved < 0 else SUB - 1, 0).astype(BF16)
        if moved < 0:
            return jnp.concatenate([edge, ref[row, : columns - SUB, :]], axis=0)
        return jnp.concatenate([ref[row, SUB:, :], edge], axis=0)

    def product(layer, group, out):
        dilation = 2**layer
        stacked = []
        for first in group:
            pieces = []
            for rho in range(4):
                ref, row = place(layer, first + (rho - 1) * dilation)
                for tap in range(3):
                    pieces.append(piece(ref, row, (tap - 1) * dilation))
            stacked.append(jnp.concatenate(pieces, axis=1))
        out[: len(group) * columns, :] = jnp.dot(
            jnp.concatenate(stacked, axis=0), weights[layer], preferred_element_type=F32
        )

    def finish(layer, group, got):
        offset = bias[layer][None, :].astype(F32)
        for k, first in enumerate(group):
            for half in range(2):
                at = first + half * 2**layer
                ref, row = place(layer, at)
                kept = piece(ref, row, 0).astype(F32)
                summed = got[k * columns : (k + 1) * columns, half * 128 : half * 128 + 128]
                value = kept + gelu(summed + offset)
                if layer + 1 == LAYERS:
                    sink(at, value)
                    continue
                if at < MARGIN:
                    value = value * low
                elif at >= MARGIN + band_rows:
                    value = value * high
                ref, row = place(layer + 1, at)
                store_row(ref, row, value, 2 ** (layer + 1))

    for k, (layer, group) in enumerate(plan):
        if k and plan[k - 1][0] == layer:
            product(layer, group, results.at[k % 2])
            finish(*plan[k - 1], results.at[(k - 1) % 2])
        else:
            if k:
                finish(*plan[k - 1], results.at[(k - 1) % 2])
            product(layer, group, results.at[k % 2])
    finish(*plan[-1], results.at[(len(plan) - 1) % 2])


def plans(band_rows):
    edge = MARGIN + band_rows
    ready = edge - 1
    whole, early, late = [], [], []
    for layer in range(LAYERS):
        dilation = 2**layer
        rows = layer_rows(layer, band_rows)
        whole += [(layer, g) for g in row_groups(rows, dilation, GROUP)]
        ready -= dilation
        first = [r for r in rows if r <= ready]
        first = first[: len(first) // (2 * dilation) * 2 * dilation]
        ready = first[-1] if first else 0
        early += [(layer, g) for g in row_groups(first, dilation, GROUP)]
        rest = [r for r in rows if r not in first]
        late += [(layer, g) for g in row_groups(rest, dilation, GROUP)]
    return whole, early, late


def pick(own, up, down, e):
    band_rows = own.shape[0]
    if e < MARGIN:
        return up, e
    if e < MARGIN + band_rows:
        return own, e - MARGIN
    return down, e - MARGIN - band_rows


def lead_one_kernel(
    own, up, down, weights, bias, field, send_up, send_down, mid_a, mid_b, results
):
    band_rows, columns = own.shape[0], up.shape[1]

    def place(layer, e):
        if layer == 0:
            return pick(own, up, down, e)
        return (mid_a, mid_b)[layer - 1], e

    def sink(e, value):
        give_row(e - MARGIN, value, field, send_up, send_down)

    conv_rows(
        plans(band_rows)[0], place, sink, weights, bias, results, band_rows, columns
    )


def early_kernel(own, up, weights, bias, top_a, top_b, results):
    band_rows, columns = own.shape[0], up.shape[1]

    def place(layer, e):
        if layer == 0:
            return pick(own, up, None, e)
        return (top_a, top_b)[layer - 1], e

    conv_rows(
        plans(band_rows)[1], place, None, weights, bias, results, band_rows, columns
    )


def table_kernel(
    gathered, conv_weight, state, owners, sea,
    weights, table, spread_state, kept_state, unspread, owner_of, sea_of,
):
    pair_weights(conv_weight, weights)
    blocks = state.shape[0]
    owner_of[...] = jnp.transpose(jnp.broadcast_to(owners[...], (128, blocks)))
    sea_of[...] = jnp.transpose(jnp.broadcast_to(sea[...], (128, blocks)))

    a = lax.broadcasted_iota(jnp.int32, (512, 512), 0)
    b = lax.broadcasted_iota(jnp.int32, (512, 512), 1)
    unspread[...] = jnp.where(a == ((b & 15) << 5) + (b >> 4), 1.0, 0.0).astype(BF16)
    spread = jnp.where(((b & 31) << 4) + (b >> 5) == a, 1.0, 0.0).astype(BF16)
    kept = jnp.dot(state[...], spread, preferred_element_type=F32).astype(BF16)
    kept_state[...] = kept
    zero = jnp.zeros((blocks, 32), BF16)
    for i in range(BH):
        cells = []
        for q in range(BW):
            at = (i * BW + q) * 32
            cells += [zero, kept[:, at : at + 32]]
        spread_state[:, i * 256 : i * 256 + 256] = jnp.concatenate(cells, axis=1)

    left = lax.broadcasted_iota(jnp.int32, (32, 128), 1) < 64
    nothing = jnp.zeros((32, 128), BF16)

    def body(owner, carry):
        pack = gathered[owner]
        other = pltpu.roll(pack.astype(F32), 64, 1).astype(BF16)

        def tap_at(t, right):
            if t < 4:
                return (other if right else pack)[t * 32 : t * 32 + 32]
            if t > 4:
                return (pack if right else other)[t * 32 - 144 : t * 32 - 112]
            first, second = (other, pack) if right else (pack, other)
            return jnp.concatenate([first[128:144], second[:16]], axis=0)

        for tap_row in range(3):
            for j in range(BW):
                for pair in range(BW // 2):
                    b = 2 * pair - j + 1
                    one = tap_at(tap_row * 3 + b, False) if 0 <= b < 3 else nothing
                    two = tap_at(tap_row * 3 + b + 1, True) if 0 <= b + 1 < 3 else nothing
                    at = tap_row * 256 + pair * 128
                    table[owner, j * 32 : j * 32 + 32, at : at + 128] = jnp.where(left, one, two)
        return carry

    lax.fori_loop(0, gathered.shape[0], body, 0)


def late_kernel(
    rotations, own, up, down, top_a, top_b, weights, bias, force, table,
    spread_state, kept_state, unspread, owner_of, sea_of,
    atmos_out, sea_state, mid_a, mid_b, results, last, joined, acc,
):
    band_rows, columns = own.shape[0], up.shape[1]
    _, early, late = plans(band_rows)
    firsts = [
        {r for l, g in early for f in g for r in (f, f + 2**l) if l == layer}
        for layer in range(LAYERS)
    ]

    def place(layer, e):
        if layer == 0:
            return pick(own, up, down, e)
        if e in firsts[layer - 1]:
            return (top_a, top_b)[layer - 1], e
        return (mid_a, mid_b)[layer - 1], e

    def sink(e, value):
        last[e - MARGIN] = value.astype(BF16)

    conv_rows(late, place, sink, weights, bias, results, band_rows, columns)

    shift = rotations[lax.axis_index("tile")]
    hot = one_hot_columns(columns, shift, True, False)
    for row in range(0, band_rows, 2):
        moved = jnp.dot(
            hot, jnp.concatenate([last[row], last[row + 1]], axis=1), preferred_element_type=F32
        )
        atmos_out[row] = moved[:, :128].astype(BF16)
        atmos_out[row + 1] = moved[:, 128:].astype(BF16)

    wide = force[...]
    none = jnp.zeros_like(wide)
    repeated = jnp.concatenate([wide, none] * BW, axis=0)
    repeated = jnp.concatenate([repeated, repeated], axis=1)
    per_half = columns // BW
    cells = lax.broadcasted_iota(jnp.int32, (columns, columns), 0)
    stored = lax.broadcasted_iota(jnp.int32, (columns, columns), 1)
    wanted = ((cells % per_half) * BW + cells // per_half + shift) & (columns - 1)
    gather = jnp.where(
        wanted == (stored % SUB) * (columns // SUB) + stored // SUB, 1.0, 0.0
    ).astype(BF16)
    lane = lax.broadcasted_iota(jnp.int32, (per_half, 256), 1) // 64
    blocks = band_rows // BH * per_half
    joined[...] = jnp.zeros_like(joined)
    for row in range(band_rows):
        both = jnp.concatenate(
            [own[row, PAD * SUB : PAD * SUB + columns, :], last[row]], axis=1
        )
        forcing = (
            0.5
            * lax.dot_general(both, repeated, (((1,), (1,)), ((), ())), preferred_element_type=F32)
        ).astype(BF16)
        spots = jnp.dot(gather, forcing, preferred_element_type=F32)
        mine = spots[:per_half]
        for q in range(1, BW):
            mine = jnp.where(lane == q, spots[q * per_half : (q + 1) * per_half], mine)
        half, i = row // BH, row % BH
        first = half * per_half
        mine = (
            mine + spread_state[first : first + per_half, i * 256 : i * 256 + 256].astype(F32)
        ).astype(BF16)
        for tap_row in range(3):
            to = i - tap_row + 1
            if 0 <= to < BH:
                joined[
                    to * blocks + first : to * blocks + first + per_half,
                    tap_row * 256 : tap_row * 256 + 256,
                ] = mine
    owner = owner_of[...]

    def body(k, carry):
        pair = jnp.concatenate([table[2 * k], table[2 * k + 1]], axis=0)
        for i in range(BH):
            here = pl.ds(i * blocks, blocks)
            got = lax.dot_general(
                joined[here, :], pair, (((1,), (1,)), ((), ())), preferred_element_type=F32
            )
            new = jnp.where(owner == 2 * k, got[:, :128], acc[here, :])
            acc[here, :] = jnp.where(owner == 2 * k + 1, got[:, 128:], new)
        return carry

    acc[...] = jnp.zeros_like(acc)
    lax.fori_loop(0, table.shape[0] // 2, body, 0)
    fresh = []
    for i in range(BH):
        kept = kept_state[:, i * 128 : i * 128 + 128].astype(F32)
        value = kept + gelu(acc[i * blocks : (i + 1) * blocks, :])
        fresh.append(jnp.where(sea_of[...] > 0, value, 0.0).astype(BF16))
    sea_state[...] = jnp.dot(
        jnp.concatenate(fresh, axis=1), unspread[...], preferred_element_type=F32
    ).astype(BF16)


def call(kernel, out_shape, scratch, specs, limit):
    return pl.pallas_call(
        kernel,
        out_shape=out_shape,
        in_specs=[pl.BlockSpec(memory_space=s) for s in specs],
        out_specs=jax.tree.map(lambda _: pl.BlockSpec(memory_space=VMEM), out_shape),
        scratch_shapes=scratch,
        compiler_params=pltpu.CompilerParams(vmem_limit_bytes=limit * 2**20),
    )


def here(*xs):
    return [pltpu.with_memory_space_constraint(x, VMEM) for x in xs]


def local(
    atmosphere, ocean_state, land_sea, owners, rotations,
    conv_weight, conv_bias, force_weight, ocean_weight,
):
    tiles = lax.axis_size("tile")
    band_rows, columns, channels = atmosphere.shape
    blocks = owners.shape[0]
    shape = jax.ShapeDtypeStruct
    up_pairs = [(i, i + 1) for i in range(tiles - 1)]
    down_pairs = [(j, i) for i, j in up_pairs]
    padded = columns + 2 * PAD * SUB
    extended = band_rows + 2 * MARGIN
    field = pltpu.VMEM((band_rows, padded, channels), BF16)
    halo = pltpu.VMEM((MARGIN, columns, channels), BF16)
    middle = pltpu.VMEM((extended, padded, channels), BF16)
    paired = pltpu.VMEM((LAYERS, 1536, 256), BF16)
    results = pltpu.VMEM((2, GROUP * columns, 256), F32)

    own, send_up, send_down = call(
        rotate_kernel, (field, halo, halo), [], [SMEM, VMEM], 8
    )(rotations, atmosphere)
    up = lax.ppermute(send_up, "tile", up_pairs)
    down = lax.ppermute(send_down, "tile", down_pairs)

    packed = call(
        pack_kernel, pltpu.VMEM((tiles, 144, 128), BF16), [], [VMEM], 4
    )(jnp.swapaxes(ocean_weight[0], 1, 2).reshape(-1, 64))
    gathered = lax.all_to_all(here(packed)[0], "tile", 0, 0, tiled=True)

    weights = call(pair_weights, paired, [], [VMEM], 4)(conv_weight)

    lead_one, send_up, send_down = call(
        lead_one_kernel, (field, halo, halo), [middle, middle, results],
        [VMEM] * 5, 16,
    )(*here(own, up, down, weights), conv_bias)

    up = lax.ppermute(send_up, "tile", up_pairs)
    down = lax.ppermute(send_down, "tile", down_pairs)

    weights, *tables = call(
        table_kernel,
        (
            paired,
            pltpu.VMEM((tiles, 128, 768), BF16),
            pltpu.VMEM((blocks, 1024), BF16),
            pltpu.VMEM((blocks, 512), BF16),
            pltpu.VMEM((512, 512), BF16),
            pltpu.VMEM((blocks, 128), jnp.int32),
            pltpu.VMEM((blocks, 128), jnp.int32),
        ),
        [], [VMEM] * 5, 8,
    )(
        *here(gathered), conv_weight, ocean_state,
        owners.reshape(1, blocks), land_sea.reshape(1, blocks),
    )
    lead_one, up, down, weights, *tables = here(lead_one, up, down, weights, *tables)
    tops = call(
        early_kernel, (middle, middle), [results], [VMEM] * 4, 16
    )(lead_one, up, weights, conv_bias)

    return call(
        late_kernel,
        (shape(atmosphere.shape, BF16), shape(ocean_state.shape, BF16)),
        [
            middle, middle, results,
            pltpu.VMEM((band_rows, columns, channels), BF16),
            pltpu.VMEM((BH * blocks, 768), BF16),
            pltpu.VMEM((BH * blocks, 128), F32),
        ],
        [SMEM] + [VMEM] * 14, 20,
    )(
        rotations, lead_one, up, down, *here(*tops), weights, conv_bias, force_weight.T, *tables
    )


def solution(mesh):
    in_specs = (
        P(("ens", "tile"), None, None),
        P(("ens", "tile"), None),
        P("tile"),
        P("tile", None),
        P(),
        P(),
        P(),
        P(),
        P("tile", None, None, None),
    )
    out_specs = (P(("ens", "tile"), None, None), P(("ens", "tile"), None))

    return jax.shard_map(local, mesh=mesh, in_specs=in_specs, out_specs=out_specs, check_vma=False)
```

```python
import jax
import jax.numpy as jnp
from jax import lax
from jax.experimental import pallas as pl
from jax.experimental.pallas import tpu as pltpu
from jax.sharding import PartitionSpec as P


LAYERS = 3
BH = 4
BW = 4
SUB = 16
PAD = 4
GROUP = 2
MARGIN = 2**LAYERS - 1
F32 = jnp.float32
BF16 = jnp.bfloat16
VMEM = pltpu.MemorySpace.VMEM
SMEM = pltpu.MemorySpace.SMEM


def gelu(x):
    half = 0.5 * x
    inner = x * (0.7978845608028654 + 0.035677408136300125 * (x * x))
    return half + half * jnp.tanh(inner)


def one_hot_columns(columns, shift, source_permuted, target_permuted):
    target = lax.broadcasted_iota(jnp.int32, (columns, columns), 0)
    source = lax.broadcasted_iota(jnp.int32, (columns, columns), 1)
    tiles = columns // SUB
    if target_permuted:
        target = (target % SUB) * tiles + target // SUB
    if source_permuted:
        source = (source % SUB) * tiles + source // SUB
    wanted = (target + shift) & (columns - 1)
    return jnp.where(wanted == source, 1.0, 0.0).astype(BF16)


def store_row(ref, row, value, reach):
    columns = value.shape[0]
    ref[row, PAD * SUB : PAD * SUB + columns, :] = value.astype(BF16)
    for k in range(reach):
        first = value[k * SUB : (k + 1) * SUB]
        at = PAD * SUB + columns + k * SUB
        ref[row, at : at + SUB, :] = pltpu.roll(first, SUB - 1, 0).astype(BF16)
        low = columns - (k + 1) * SUB
        last = value[low : low + SUB]
        at = PAD * SUB - (k + 1) * SUB
        ref[row, at : at + SUB, :] = pltpu.roll(last, 1, 0).astype(BF16)


def layer_rows(layer, band_rows):
    used = 2 ** (layer + 1) - 1
    return list(range(used, band_rows + 2 * MARGIN - used))


def row_groups(rows, dilation, size):
    rows = set(rows)
    firsts = []
    while rows:
        r = min(rows)
        firsts.append(r)
        rows -= {r, r + dilation}
    return [firsts[k : k + size] for k in range(0, len(firsts), size)]


def flipped():
    return lax.axis_index("tile") % 2 == 0


def far_tile():
    tile = lax.axis_index("tile")
    return tile + jnp.where(tile % 2 == 0, -1, 1)


def turn(index, count):
    return jnp.where(flipped(), count - 1 - index, index)


def give_row(row, value, field, send_near, send_far):
    store_row(field, row, value, 1)
    if row < MARGIN:
        send_near[MARGIN - 1 - row] = value.astype(BF16)
    if row > 0:
        send_far[MARGIN - row] = value.astype(BF16)


def rotate_kernel(
    rotations, atmosphere, field, send_near, send_far, own, shifts, own_sem, shift_sem
):
    get_shifts = pltpu.make_async_copy(rotations, shifts, shift_sem)
    get_own = pltpu.make_async_copy(atmosphere, own, own_sem)
    get_shifts.start()
    get_own.start()
    band_rows, columns = own.shape[0], own.shape[1]
    get_shifts.wait()
    hot = one_hot_columns(columns, -shifts[lax.axis_index("tile")], False, True)
    get_own.wait()
    for k in range(0, band_rows, 2):
        pair = [own[turn(k + half, band_rows)] for half in range(2)]
        moved = jnp.dot(hot, jnp.concatenate(pair, axis=1), preferred_element_type=F32)
        for half in range(2):
            give_row(k + half, moved[:, half * 128 : half * 128 + 128], field, send_near, send_far)


def pack_kernel(ocean_weight, packed):
    taps = ocean_weight[...].astype(F32)
    none = jnp.zeros((32, 32), F32)
    for tap_row in range(3):
        for half in range(2):
            cells = [
                taps[(tap_row * 3 + b) * 32 : (tap_row * 3 + b) * 32 + 32, half * 32 : half * 32 + 32]
                for b in range(3)
            ]
            at = (tap_row * 2 + half) * 32
            packed[0, at : at + 32, :] = jnp.concatenate(cells + [none], axis=1).astype(BF16)


def pair_weights(conv_weight, weights):
    zero = jnp.zeros((384, 128), BF16)
    for layer in range(LAYERS):
        for half in range(2):
            at = (1 - half) * 1152
            weights[layer, at : at + 384, half * 128 : half * 128 + 128] = zero
            for tap_row in range(3):
                for tap in range(3):
                    at = half * 384 + tap_row * 384 + tap * 128
                    weights[layer, at : at + 128, half * 128 : half * 128 + 128] = conv_weight[
                        layer, turn(tap_row, 3) * 3 + tap
                    ]


def conv_rows(plan, place, sink, weights, bias, results, band_rows, columns):
    reach = far_tile()
    inside = (reach >= 0) & (reach < lax.axis_size("tile"))
    inside = jnp.where(inside, 1.0, 0.0).astype(F32)

    def piece(ref, row, moved):
        padded = ref.shape[1] > columns
        if padded or moved == 0:
            start = (PAD * SUB if padded else 0) + moved * SUB
            return ref[row, start : start + columns, :]
        edge = ref[row, columns - SUB :, :] if moved < 0 else ref[row, :SUB, :]
        edge = pltpu.roll(edge.astype(F32), 1 if moved < 0 else SUB - 1, 0).astype(BF16)
        if moved < 0:
            return jnp.concatenate([edge, ref[row, : columns - SUB, :]], axis=0)
        return jnp.concatenate([ref[row, SUB:, :], edge], axis=0)

    def product(layer, group, out):
        dilation = 2**layer
        stacked = []
        for first in group:
            pieces = []
            for rho in range(4):
                ref, row = place(layer, first + (rho - 1) * dilation)
                for tap in range(3):
                    pieces.append(piece(ref, row, (tap - 1) * dilation))
            stacked.append(jnp.concatenate(pieces, axis=1))
        out[: len(group) * columns, :] = jnp.dot(
            jnp.concatenate(stacked, axis=0), weights[layer], preferred_element_type=F32
        )

    def finish(layer, group, got):
        offset = bias[layer][None, :].astype(F32)
        for k, first in enumerate(group):
            for half in range(2):
                at = first + half * 2**layer
                ref, row = place(layer, at)
                kept = piece(ref, row, 0).astype(F32)
                summed = got[k * columns : (k + 1) * columns, half * 128 : half * 128 + 128]
                value = kept + gelu(summed + offset)
                if layer + 1 == LAYERS:
                    sink(at, value)
                    continue
                if at >= MARGIN + band_rows:
                    value = value * inside
                ref, row = place(layer + 1, at)
                store_row(ref, row, value, 2 ** (layer + 1))

    for k, (layer, group) in enumerate(plan):
        if k and plan[k - 1][0] == layer:
            product(layer, group, results.at[k % 2])
            finish(*plan[k - 1], results.at[(k - 1) % 2])
        else:
            if k:
                finish(*plan[k - 1], results.at[(k - 1) % 2])
            product(layer, group, results.at[k % 2])
    finish(*plan[-1], results.at[(len(plan) - 1) % 2])


def plans(band_rows):
    edge = MARGIN + band_rows
    ready = edge - 1
    early, late = [], []
    for layer in range(LAYERS):
        dilation = 2**layer
        rows = layer_rows(layer, band_rows)
        ready -= dilation
        first = [r for r in rows if r <= ready]
        first = first[: len(first) // (2 * dilation) * 2 * dilation]
        ready = first[-1] if first else 0
        early += [(layer, g) for g in row_groups(first, dilation, GROUP)]
        rest = [r for r in rows if r not in first]
        late += [(layer, g) for g in row_groups(rest, dilation, GROUP)]
    return early, late


def pick(own, near, far, e):
    band_rows = own.shape[0]
    if e < MARGIN:
        return near, e
    if e < MARGIN + band_rows:
        return own, e - MARGIN
    return far, e - MARGIN - band_rows


def early_kernel(own, near, weights, bias, top_a, top_b, results):
    band_rows, columns = own.shape[0], near.shape[1]

    def place(layer, e):
        if layer == 0:
            return pick(own, near, None, e)
        return (top_a, top_b)[layer - 1], e

    conv_rows(plans(band_rows)[0], place, None, weights, bias, results, band_rows, columns)


def late_rows(own, near, far, top_a, top_b, weights, bias, mid_a, mid_b, results, sink):
    band_rows, columns = own.shape[0], near.shape[1]
    early, late = plans(band_rows)
    firsts = [
        {r for l, g in early for f in g for r in (f, f + 2**l) if l == layer}
        for layer in range(LAYERS)
    ]

    def place(layer, e):
        if layer == 0:
            return pick(own, near, far, e)
        if e in firsts[layer - 1]:
            return (top_a, top_b)[layer - 1], e
        return (mid_a, mid_b)[layer - 1], e

    conv_rows(late, place, sink, weights, bias, results, band_rows, columns)


def late_one_kernel(
    own, near, far, top_a, top_b, weights, bias, field, send_near, send_far, *scratch
):
    def sink(e, value):
        give_row(e - MARGIN, value, field, send_near, send_far)

    late_rows(own, near, far, top_a, top_b, weights, bias, *scratch, sink)


def by_owner(joined, table, owner_of, acc):
    tiles = table.shape[0]
    blocks = owner_of.shape[0]
    bits = tiles.bit_length() - 1
    tile = lax.axis_index("tile")

    def owner_at(slot):
        mirrored = sum(((slot >> k) & 1) << (bits - 1 - k) for k in range(bits))
        return tile ^ mirrored

    def body(k, carry):
        pair = jnp.concatenate([table[2 * k], table[2 * k + 1]], axis=0)
        got = lax.dot_general(
            joined[...], pair, (((1,), (1,)), ((), ())), preferred_element_type=F32
        )
        first = owner_of[...] == owner_at(2 * k)
        second = owner_of[...] == owner_at(2 * k + 1)
        for i in range(BH):
            rows = slice(i * blocks, i * blocks + blocks)
            new = jnp.where(first, got[rows, :128], acc[rows, :])
            acc[rows, :] = jnp.where(second, got[rows, 128:], new)
        return carry

    acc[...] = jnp.zeros_like(acc)
    lax.fori_loop(0, tiles // 2, body, 0, unroll=tiles <= 16)


def table_kernel(*refs):
    *pieces, state, owners, sea = refs[:-8]
    table, kept_state, unspread, owner_of, sea_of, acc, joined, state_table = refs[-8:]
    blocks = state.shape[0]
    owner_of[...] = jnp.transpose(jnp.broadcast_to(owners[...], (128, blocks)))
    sea_of[...] = jnp.transpose(jnp.broadcast_to(sea[...], (128, blocks)))

    a = lax.broadcasted_iota(jnp.int32, (512, 512), 0)
    b = lax.broadcasted_iota(jnp.int32, (512, 512), 1)
    unspread[...] = jnp.where(a == ((b & 15) << 5) + (b >> 4), 1.0, 0.0).astype(BF16)
    spread = jnp.where(((b & 31) << 4) + (b >> 5) == a, 1.0, 0.0).astype(BF16)
    kept = jnp.dot(state[...], spread, preferred_element_type=F32).astype(BF16)
    kept_state[...] = kept
    none = jnp.zeros((blocks, 128), BF16)
    for i in range(BH):
        for tap_row in range(3):
            at = i + tap_row - 1
            joined[i * blocks : (i + 1) * blocks, tap_row * 128 : tap_row * 128 + 128] = (
                kept[:, at * 128 : at * 128 + 128] if 0 <= at < BH else none
            )

    lane = lax.broadcasted_iota(jnp.int32, (32, 128), 1)
    base = 0
    for piece in pieces:

        def body(k, carry, piece=piece, base=base):
            for tap_row in range(3):
                for half, to in enumerate((table, state_table)):
                    at = (tap_row * 2 + half) * 32
                    strip = piece[k, at : at + 32, :].astype(F32)
                    for j in range(BW):
                        moved = strip if j == 1 else pltpu.roll(strip, 32 * (j - 1) % 128, 1)
                        if j == 0:
                            moved = jnp.where(lane < 96, moved, 0.0)
                        if j == 3:
                            moved = jnp.where(lane >= 32, moved, 0.0)
                        to[base + k, j * 32 : j * 32 + 32, tap_row * 128 : tap_row * 128 + 128] = (
                            moved.astype(BF16)
                        )
            return carry

        lax.fori_loop(0, piece.shape[0], body, 0)
        base += piece.shape[0]
    by_owner(joined, state_table, owner_of, acc)


def late_two_kernel(
    rotations, own, near, far, top_a, top_b, weights, bias, force,
    table, kept_state, unspread, owner_of, sea_of, state_part,
    atmos_out, sea_state, mid_a, mid_b, results, last, joined, acc,
):
    band_rows, columns = own.shape[0], near.shape[1]

    def sink(e, value):
        last[e - MARGIN] = value.astype(BF16)

    late_rows(own, near, far, top_a, top_b, weights, bias, mid_a, mid_b, results, sink)

    shift = rotations[lax.axis_index("tile")]
    repeated = jnp.concatenate([force[...]] * BW, axis=0)
    repeated = jnp.concatenate([repeated, repeated], axis=1)
    per_half = columns // BW
    cells = lax.broadcasted_iota(jnp.int32, (columns, columns), 0)
    stored = lax.broadcasted_iota(jnp.int32, (columns, columns), 1)
    wanted = ((cells % per_half) * BW + cells // per_half + shift) & (columns - 1)
    gather = jnp.where(
        wanted == (stored % SUB) * (columns // SUB) + stored // SUB, 1.0, 0.0
    ).astype(BF16)
    lane = lax.broadcasted_iota(jnp.int32, (per_half, 256), 1) % 128 // 32
    blocks = band_rows // BH * per_half
    joined[...] = jnp.zeros_like(joined)
    for row in range(0, band_rows, 2):
        forcing = []
        for k in range(2):
            at = turn(row + k, band_rows)
            both = jnp.concatenate(
                [own[at, PAD * SUB : PAD * SUB + columns, :], last[at]], axis=1
            )
            summed = lax.dot_general(
                both, repeated, (((1,), (1,)), ((), ())), preferred_element_type=F32
            )
            forcing.append((0.5 * summed).astype(BF16))
        spots = jnp.dot(gather, jnp.concatenate(forcing, axis=1), preferred_element_type=F32)
        mine = spots[:per_half]
        for q in range(1, BW):
            mine = jnp.where(lane == q, spots[q * per_half : (q + 1) * per_half], mine)
        mine = mine.astype(BF16)
        first = row // BH * per_half
        for k in range(2):
            for tap_row in range(3):
                to = row % BH + k - tap_row + 1
                if 0 <= to < BH:
                    joined[
                        to * blocks + first : to * blocks + first + per_half,
                        tap_row * 128 : tap_row * 128 + 128,
                    ] = mine[:, k * 128 : k * 128 + 128]
    by_owner(joined, table, owner_of, acc)

    hot = one_hot_columns(columns, shift, True, False)
    for row in range(0, band_rows, 2):
        pair = [last[turn(row + half, band_rows)] for half in range(2)]
        moved = jnp.dot(hot, jnp.concatenate(pair, axis=1), preferred_element_type=F32)
        atmos_out[row] = moved[:, :128].astype(BF16)
        atmos_out[row + 1] = moved[:, 128:].astype(BF16)

    fresh = []
    for i in range(BH):
        rows = slice(i * blocks, i * blocks + blocks)
        kept = kept_state[:, i * 128 : i * 128 + 128].astype(F32)
        value = kept + gelu(acc[rows, :] + state_part[rows, :])
        fresh.append(jnp.where(sea_of[...] > 0, value, 0.0).astype(BF16))
    sea_state[...] = jnp.dot(
        jnp.concatenate(fresh, axis=1), unspread[...], preferred_element_type=F32
    ).astype(BF16)


def call(kernel, out_shape, scratch, specs, limit):
    return pl.pallas_call(
        kernel,
        out_shape=out_shape,
        in_specs=[pl.BlockSpec(memory_space=s) for s in specs],
        out_specs=jax.tree.map(lambda _: pl.BlockSpec(memory_space=VMEM), out_shape),
        scratch_shapes=scratch,
        compiler_params=pltpu.CompilerParams(vmem_limit_bytes=limit * 2**20),
    )


def here(*xs):
    return [pltpu.with_memory_space_constraint(x, VMEM) for x in xs]


def exchange(send_near, send_far, tiles):
    far_pairs = [(t, t + 1 if t % 2 else t - 1) for t in range(1, tiles - 1)]
    far = lax.ppermute(send_far, "tile", far_pairs)
    near = lax.ppermute(send_near, "tile", [(t, t ^ 1) for t in range(tiles)])
    return here(near, far)


def local(
    atmosphere, ocean_state, land_sea, owners, rotations,
    conv_weight, conv_bias, force_weight, ocean_weight,
):
    tiles = lax.axis_size("tile")
    band_rows, columns, channels = atmosphere.shape
    blocks = owners.shape[0]
    shape = jax.ShapeDtypeStruct
    padded = columns + 2 * PAD * SUB
    extended = band_rows + 2 * MARGIN
    field = pltpu.VMEM((band_rows, padded, channels), BF16)
    halo = pltpu.VMEM((MARGIN, columns, channels), BF16)
    middle = pltpu.VMEM((extended, padded, channels), BF16)
    results = pltpu.VMEM((2, GROUP * columns, 256), F32)

    own, send_near, send_far = call(
        rotate_kernel, (field, halo, halo),
        [
            pltpu.VMEM(atmosphere.shape, BF16),
            pltpu.SMEM(rotations.shape, jnp.int32),
            pltpu.SemaphoreType.DMA,
            pltpu.SemaphoreType.DMA,
        ],
        [pl.ANY, pl.ANY], 8,
    )(rotations, atmosphere)
    near, far = exchange(send_near, send_far, tiles)

    pieces = [
        call(pack_kernel, pltpu.VMEM((1, 192, 128), BF16), [], [VMEM], 4)(
            jnp.swapaxes(ocean_weight[0], 1, 2).reshape(-1, 64)
        )
    ]
    have = pieces[0]
    step = tiles // 2
    while step:
        pieces.append(lax.ppermute(have, "tile", [(t, t ^ step) for t in range(tiles)]))
        if step > 1:
            have = jnp.concatenate([have, pieces[-1]], axis=0)
        step //= 2

    weights = call(pair_weights, pltpu.VMEM((LAYERS, 1536, 256), BF16), [], [VMEM], 4)(conv_weight)
    own, weights = here(own, weights)

    def early(own, near):
        return here(
            *call(early_kernel, (middle, middle), [results], [VMEM] * 4, 16)(
                own, near, weights, conv_bias
            )
        )

    tops = early(own, near)
    own, send_near, send_far = call(
        late_one_kernel, (field, halo, halo), [middle, middle, results],
        [VMEM] * 7, 16,
    )(own, near, far, *tops, weights, conv_bias)
    (own,) = here(own)
    near, far = exchange(send_near, send_far, tiles)
    tops = early(own, near)

    tables = call(
        table_kernel,
        (
            pltpu.VMEM((tiles, 128, 384), BF16),
            pltpu.VMEM((blocks, 512), BF16),
            pltpu.VMEM((512, 512), BF16),
            pltpu.VMEM((blocks, 128), jnp.int32),
            pltpu.VMEM((blocks, 128), jnp.int32),
            pltpu.VMEM((BH * blocks, 128), F32),
        ),
        [pltpu.VMEM((BH * blocks, 384), BF16), pltpu.VMEM((tiles, 128, 384), BF16)],
        [VMEM] * (len(pieces) + 3), 8 + tiles // 4,
    )(*here(*pieces), ocean_state, owners.reshape(1, blocks), land_sea.reshape(1, blocks))

    return call(
        late_two_kernel,
        (shape(atmosphere.shape, BF16), shape(ocean_state.shape, BF16)),
        [
            middle, middle, results,
            pltpu.VMEM((band_rows, columns, channels), BF16),
            pltpu.VMEM((BH * blocks, 384), BF16),
            pltpu.VMEM((BH * blocks, 128), F32),
        ],
        [SMEM] + [VMEM] * 14, 20,
    )(
        rotations, own, near, far, *tops, weights, conv_bias, force_weight.T, *here(*tables)
    )


def solution(mesh):
    in_specs = (
        P(("ens", "tile"), None, None),
        P(("ens", "tile"), None),
        P("tile"),
        P("tile", None),
        P(),
        P(),
        P(),
        P(),
        P("tile", None, None, None),
    )
    out_specs = (P(("ens", "tile"), None, None), P(("ens", "tile"), None))

    return jax.shard_map(local, mesh=mesh, in_specs=in_specs, out_specs=out_specs, check_vma=False)
```
